256 devices in a mesh: tm: 8 (over z_hi, x), space: 32 (over y, z_lo, core).
Axes of the slice: x: 4, y: 4, z: 8 (z_hi: 2, z_lo: 4; z = z_hi * 4 + z_lo), core: 2. Of those that a mesh axis runs over, the one named last changes fastest.
Arguments:
- eof_basis: bfloat16 [262144, 256], P('space'), may hold values from -0.01171875 to 0.01171875
- snapshots: bfloat16 [262144, 512], P('space', 'tm'), may hold values from -6 to 6
- inverse_energy: float32 [256], replicated, may hold values from 0.022097087 to 0.22097087
- eigen_vectors: bfloat16 [256, 512], replicated, may hold values from -0.375 to 0.375
Outputs:
- reduced_operator: float32 [256, 256], replicated
- rebuilt_modes: bfloat16 [512, 262144], P('tm', 'space')
The draws below stay inside these ranges and needn't reach their ends.
All inputs are finite; a program needn't handle non-finite values.
Results may differ from the reference program's by a relative error of at most 0.0049.
Values may be sent and summed in bfloat16 or wider, within the bound.
A program may use at most 64 MiB of HBM per device.

```python
import math
import jax
import jax.numpy as jnp
from jax import lax

R = 256
CELLS = 262144
HOURS = 512


def block_levels(rng, shape, split, least, top_value):
    level = 1.0
    for dim, parts in split:
        draws = jax.random.uniform(jax.random.fold_in(jax.random.fold_in(rng, 6), dim), (parts,), jnp.float32, least / len(split), top_value / len(split))
        level = level * jnp.repeat(jnp.exp(draws), shape[dim] // parts).reshape((-1,) + (1,) * (len(shape) - 1 - dim))
    return level


def gaussian(own_key, shape, width, bound, pieces=(), held_as=jnp.bfloat16):
    drawn = jax.random.normal(own_key, shape, jnp.float32) * width
    if len(pieces) > 0:
        drawn = block_levels(own_key, shape, pieces, -0.22, 0.18) * drawn
    return jnp.clip(drawn, min=-bound, max=bound).astype(held_as)


def setup_inputs(seed: int = 0) -> dict:
    keys = jax.random.split(jax.random.key(seed), 5)
    return {
        "eof_basis": gaussian(keys[0], (CELLS, R), CELLS ** -0.5, 0.01171875, ((0, 32),)),
        "snapshots": gaussian(keys[1], (CELLS, HOURS), 1.0, 6.0, ((0, 32), (1, 8))),
        "inverse_energy": jnp.clip(jnp.exp(jax.random.uniform(keys[2], (R,), jnp.float32, math.log(0.022097087), math.log(0.22097087))), 0.022097087, 0.22097087),
        "eigen_vectors": gaussian(keys[3], (R, 2 * R), R ** -0.5, 0.375),
    }


def reference(eof_basis, snapshots, inverse_energy, eigen_vectors):
    coeffs = lax.dot_general(eof_basis, snapshots, (((0,), (0,)), ((), ())), preferred_element_type=jnp.float32)
    lagged = jnp.concatenate([jnp.zeros((coeffs.shape[0], 1), jnp.float32), coeffs[:, :-1]], axis=1)
    scaled = lagged * inverse_energy[:, None]
    reduced_operator = jnp.dot(coeffs, scaled.T, precision=lax.Precision.HIGHEST)
    hour_weights = jnp.dot(scaled.T, eigen_vectors.astype(jnp.float32), precision=lax.Precision.HIGHEST).astype(jnp.bfloat16)
    modes = lax.dot_general(hour_weights, snapshots, (((0,), (1,)), ((), ())), preferred_element_type=jnp.float32)
    return reduced_operator, modes.astype(jnp.bfloat16)
```

```python
import functools

import jax
import jax.numpy as jnp
from jax import lax
from jax.experimental import pallas as pl
from jax.experimental.pallas import tpu as pltpu
from jax.sharding import PartitionSpec as P

MESH = pl.DeviceIdType.MESH
F32, BF16 = jnp.float32, jnp.bfloat16

NX, NY, NZ, NZL, NCORE = 4, 4, 8, 4, 2
CHUNKS = 4
K_CHUNKS = 4
PRODUCT = (((1,), (0,)), ((), ()))
ALONG_LAST = (((1,), (1,)), ((), ()))
ALONG_FIRST = (((0,), (0,)), ((), ()))


def dot(a, b, dims=PRODUCT):
    return lax.dot_general(a, b, dims, preferred_element_type=F32)


def two_parts(a):
    high = a.astype(BF16)
    return high, (a - high.astype(F32)).astype(BF16)


def kernel(
    eof, snap, energy, vectors, operator, modes,
    eof_v, snap_v, vec_v, vec_t, parts, from_plane, from_column, total, coeffs,
    gathered, weights, rebuilt, operator_v, energy_v,
    load_sem, store_sem, send_sem, plane_sem, column_sem, x_sem, y_sem, core_sem,
    snap_sem, modes_sem,
):
    tm, space = lax.axis_index("tm"), lax.axis_index("space")
    zh, x = tm // NX, tm % NX
    y, zl, core = space // 8, (space // 2) % NZL, space % 2
    z = zh * NZL + zl
    hours, cells = snap.shape
    rank = eof.shape[1]
    piece = cells // 8
    width = piece // CHUNKS
    depth = cells // K_CHUNKS

    def at(x_, y_, z_, core_):
        return ((z_ // NZL) * NX + x_, y_ * 8 + (z_ % NZL) * 2 + core_)

    mine = y * 2 + core
    plane = [(mine + d) % 8 for d in range(1, 8)]
    plane_peers = [at(x, q // 2, z, q % 2) for q in plane]
    column_peers = [at(x, y, (z + d) % NZ, core) for d in range(1, NZ)]
    x_peers = [at((x + d) % NX, y, z, core) for d in range(1, NX)]
    y_peers = [at(x, (y + d) % NY, z, core) for d in range(1, NY)]
    other_core = at(x, y, z, 1 - core)
    far_peers = [at((x + d) % NX, y, (z + 2 + 4 * s) % NZ, core) for d in range(1, NX) for s in range(2)]

    barrier = pltpu.get_barrier_semaphore()
    peers = plane_peers + column_peers + x_peers + far_peers
    for peer in peers:
        pl.semaphore_signal(barrier, inc=1, device_id=peer, device_id_type=MESH)

    def load(source, target, i):
        copy = pltpu.make_async_copy(source, target, load_sem.at[i])
        copy.start()
        return copy

    snap_load = load(snap, snap_v, 0)
    eof_loads = [
        load(eof.at[pl.ds(k * depth, depth), :], eof_v.at[pl.ds(k * depth, depth), :], 1 + k)
        for k in range(K_CHUNKS)
    ]
    vec_load = load(vectors, vec_v, 1 + K_CHUNKS)
    energy_load = load(energy, energy_v, 2 + K_CHUNKS)

    sent = []

    def send(source, target, receive, peer, i):
        copy = pltpu.make_async_remote_copy(
            src_ref=source, dst_ref=target, send_sem=send_sem.at[i], recv_sem=receive,
            device_id=peer, device_id_type=MESH,
        )
        copy.start()
        sent.append(copy)

    def arrived(ref, sem):
        pltpu.make_async_copy(ref, ref, sem).wait()

    def send_snapshots(c):
        for d in range(NX):
            for s in range(2):
                x_, z_ = (x + d) % NX, (zl + 2 + 4 * s) % NZ
                start = pl.multiple_of((x_ * 2 + s) * piece + c * width, width)
                send(
                    snap.at[:, pl.ds(start, width)],
                    gathered.at[c, pl.ds(pl.multiple_of(tm * hours, hours), hours), :],
                    snap_sem.at[c], at(x_, y, z_, core), len(sent),
                )

    def project(k):
        eof_loads[k].wait()
        return dot(snap_v[:, k * depth:(k + 1) * depth], eof_v[k * depth:(k + 1) * depth, :])

    snap_load.wait()
    partial = project(0)
    partial += project(1)
    pl.semaphore_wait(barrier, len(peers))
    send_snapshots(0)
    for k in range(2, K_CHUNKS):
        partial += project(k)
    for q in range(8):
        parts[q] = partial[q * 8:(q + 1) * 8, :]

    for q, peer in zip(plane, plane_peers):
        send(parts.at[q], from_plane.at[mine], plane_sem, peer, len(sent))
    from_plane[mine] = parts[mine]
    vec_load.wait()
    vec_t[...] = vec_v[...].T
    arrived(from_plane.at[pl.ds(0, 7)], plane_sem)
    value = from_plane[0]
    for q in range(1, 8):
        value += from_plane[q]

    total[...] = value
    for peer in column_peers:
        send(total, from_column.at[z], column_sem, peer, len(sent))
    send_snapshots(1)
    from_column[z] = value
    arrived(from_column.at[pl.ds(0, 7)], column_sem)
    for h in range(2):
        value = from_column[h * NZL]
        for i in range(1, NZL):
            value += from_column[h * NZL + i]
        coeffs[core, y, x, h] = value

    for peer in x_peers:
        send(coeffs.at[core, y, x], coeffs.at[core, y, x], x_sem, peer, len(sent))
    send_snapshots(2)
    send_snapshots(3)
    arrived(coeffs.at[0, 0, pl.ds(0, 3)], x_sem)
    for peer in y_peers:
        send(coeffs.at[core, y], coeffs.at[core, y], y_sem, peer, len(sent))
    arrived(coeffs.at[0, pl.ds(0, 3)], y_sem)
    send(coeffs.at[core], coeffs.at[core], core_sem, other_core, len(sent))
    arrived(coeffs.at[0], core_sem)

    rows = [
        coeffs[c_, y_, x_, h]
        for h in range(2) for x_ in range(NX) for y_ in range(NY) for c_ in range(NCORE)
    ]
    whole = jnp.concatenate(rows, axis=0)
    first = lax.broadcasted_iota(jnp.int32, whole.shape, 0) == 0
    energy_load.wait()
    scaled = jnp.where(first, 0.0, pltpu.roll(whole, 1, 0)) * energy_v[...]
    scaled_high, scaled_low = two_parts(scaled)
    weights[...] = (
        dot(vec_t[...], scaled_high, ALONG_LAST) + dot(vec_t[...], scaled_low, ALONG_LAST)
    ).astype(BF16)

    owner_zl = (z + 2) % NZL
    side = ((z + 6 - owner_zl) % NZ) // 4
    owner_space = y * 8 + owner_zl * 2 + core
    for c in range(CHUNKS):
        arrived(gathered.at[c], snap_sem.at[c])
        rebuilt[c] = dot(weights[...], gathered[c]).astype(BF16)
        start = pl.multiple_of((x * 2 + side) * piece + c * width, width)
        for d in range(8):
            to = (tm + d) % 8
            send(
                rebuilt.at[c, pl.ds(pl.multiple_of(to * hours, hours), hours), :],
                modes.at[:, pl.ds(start, width)],
                modes_sem, (to, owner_space), len(sent),
            )

    whole_high, whole_low = two_parts(whole)
    operator_v[...] = (
        dot(whole_high, scaled_high, ALONG_FIRST)
        + dot(whole_high, scaled_low, ALONG_FIRST)
        + dot(whole_low, scaled_high, ALONG_FIRST)
    )
    store = pltpu.make_async_copy(operator_v, operator, store_sem)
    store.start()

    for copy in sent:
        copy.wait_send()
    store.wait()
    arrived(modes, modes_sem)


def per_device(eof_basis, snapshots, inverse_energy, eigen_vectors):
    cells, rank = eof_basis.shape
    hours = snapshots.shape[1]
    all_modes = eigen_vectors.shape[1]
    piece = cells // 8
    width = piece // CHUNKS
    anywhere = pl.BlockSpec(memory_space=pl.ANY)
    sends = 8 * CHUNKS * 2 + 7 + 7 + 3 + 3 + 1
    return pl.pallas_call(
        kernel,
        out_shape=(
            jax.ShapeDtypeStruct((rank, rank), F32),
            jax.ShapeDtypeStruct((hours, cells), BF16),
        ),
        in_specs=[anywhere] * 4,
        out_specs=(anywhere, anywhere),
        scratch_shapes=[
            pltpu.VMEM((cells, rank), BF16),
            pltpu.VMEM((hours, cells), BF16),
            pltpu.VMEM((rank, all_modes), BF16),
            pltpu.VMEM((all_modes, rank), BF16),
            pltpu.VMEM((8, 8, rank), F32),
            pltpu.VMEM((8, 8, rank), F32),
            pltpu.VMEM((NZ, 8, rank), F32),
            pltpu.VMEM((8, rank), F32),
            pltpu.VMEM((NCORE, NY, NX, 2, 8, rank), F32),
            pltpu.VMEM((CHUNKS, 8 * hours, width), BF16),
            pltpu.VMEM((all_modes, 8 * hours), BF16),
            pltpu.VMEM((CHUNKS, all_modes, width), BF16),
            pltpu.VMEM((rank, rank), F32),
            pltpu.VMEM((1, rank), F32),
            pltpu.SemaphoreType.DMA((3 + K_CHUNKS,)),
            pltpu.SemaphoreType.DMA,
            pltpu.SemaphoreType.DMA((sends,)),
            pltpu.SemaphoreType.DMA,
            pltpu.SemaphoreType.DMA,
            pltpu.SemaphoreType.DMA,
            pltpu.SemaphoreType.DMA,
            pltpu.SemaphoreType.DMA,
            pltpu.SemaphoreType.DMA((CHUNKS,)),
            pltpu.SemaphoreType.DMA,
        ],
        compiler_params=pltpu.CompilerParams(
            collective_id=0, has_side_effects=True, vmem_limit_bytes=60 * 1024 * 1024
        ),
    )(eof_basis, snapshots.T, inverse_energy.reshape(1, rank), eigen_vectors)


def solution(mesh):
    in_specs = (P("space", None), P("space", "tm"), P(), P())
    out_specs = (P(), P("tm", "space"))
    return jax.shard_map(
        per_device, mesh=mesh, in_specs=in_specs, out_specs=out_specs, check_vma=False
    )
```

```python
import functools

import jax
import jax.numpy as jnp
from jax import lax
from jax.experimental import pallas as pl
from jax.experimental.pallas import tpu as pltpu
from jax.sharding import PartitionSpec as P

MESH = pl.DeviceIdType.MESH
F32, BF16 = jnp.float32, jnp.bfloat16

NX, NY, NZ, NZL, NCORE = 4, 4, 8, 4, 2
CHUNKS = 4
K_CHUNKS = 4
PRODUCT = (((1,), (0,)), ((), ()))
ALONG_LAST = (((1,), (1,)), ((), ()))
ALONG_FIRST = (((0,), (0,)), ((), ()))


def dot(a, b, dims=PRODUCT):
    return lax.dot_general(a, b, dims, preferred_element_type=F32)


def two_parts(a):
    high = a.astype(BF16)
    return high, (a - high.astype(F32)).astype(BF16)


def kernel(
    eof, snap, energy, vectors, operator, modes,
    eof_v, snap_v, vec_v, vec_t, parts, from_plane, from_column, total, coeffs,
    gathered, weights, rebuilt, energy_v,
    load_sem, sent_sem, plane_sem, column_sem, x_sem, y_sem, core_sem,
    snap_sem, modes_sem,
):
    hours, cells = snap.shape
    piece = cells // 8
    width = piece // CHUNKS
    depth = cells // K_CHUNKS

    def load(source, target, i):
        copy = pltpu.make_async_copy(source, target, load_sem.at[i])
        copy.start()
        return copy

    snap_load = load(snap, snap_v, 0)
    eof_loads = [
        load(eof.at[pl.ds(k * depth, depth), :], eof_v.at[pl.ds(k * depth, depth), :], 1 + k)
        for k in range(K_CHUNKS)
    ]
    vec_load = load(vectors, vec_v, 1 + K_CHUNKS)
    energy_load = load(energy, energy_v, 2 + K_CHUNKS)

    tm, space = lax.axis_index("tm"), lax.axis_index("space")
    zh, x = tm >> 2, tm & 3
    y, zl, core = space >> 3, (space >> 1) & 3, space & 1
    z = zh * NZL + zl

    def at(x_, y_, z_, core_):
        return ((z_ & 4) + x_, y_ * 8 + (z_ & 3) * 2 + core_)

    mine = y * 2 + core
    plane = [mine ^ d for d in range(1, 8)]
    plane_peers = [at(x, q >> 1, z, q & 1) for q in plane]
    column_peers = [at(x, y, z ^ d, core) for d in range(1, NZ)]
    xs = [x ^ d for d in range(NX)]
    x_peers = [at(x_, y, z, core) for x_ in xs[1:]]
    y_peers = [at(x, y ^ d, z, core) for d in range(1, NY)]
    other_core = at(x, y, z, core ^ 1)
    far = [(zl + 2) & 7, (zl + 6) & 7]
    far_peers = [[at(x_, y, z_, core) for z_ in far] for x_ in xs]

    barrier = pltpu.get_barrier_semaphore()
    peers = far_peers[2] + far_peers[1] + far_peers[3] + column_peers + plane_peers + x_peers
    for peer in peers:
        pl.semaphore_signal(barrier, inc=1, device_id=peer, device_id_type=MESH)

    def send(source, target, receive, peer, group):
        pltpu.make_async_remote_copy(
            src_ref=source, dst_ref=target, send_sem=sent_sem.at[group], recv_sem=receive,
            device_id=peer, device_id_type=MESH,
        ).start()

    def passed(ref, sem):
        pltpu.make_async_copy(ref, ref, sem).wait()

    def send_snapshots(c):
        for d in range(NX):
            for s in range(2):
                start = pl.multiple_of((xs[d] * 2 + s) * piece + c * width, width)
                send(
                    snap.at[:, pl.ds(start, width)],
                    gathered.at[c, pl.ds(pl.multiple_of(tm * hours, hours), hours), :],
                    snap_sem.at[c], far_peers[d][s], 5 + c,
                )

    snap_load.wait()
    partial = None
    for k in range(K_CHUNKS):
        eof_loads[k].wait()
        term = dot(snap_v[:, k * depth:(k + 1) * depth], eof_v[k * depth:(k + 1) * depth, :])
        partial = term if partial is None else partial + term
    for q in range(8):
        parts[q] = partial[q * 8:(q + 1) * 8, :]

    pl.semaphore_wait(barrier, len(peers))
    send_snapshots(0)

    for q, peer in zip(plane, plane_peers):
        send(parts.at[q], from_plane.at[mine], plane_sem, peer, 0)
    from_plane[mine] = parts[mine]
    vec_load.wait()
    vec_t[...] = vec_v[...].T
    passed(from_plane.at[pl.ds(0, 7)], plane_sem)
    value = from_plane[0]
    for q in range(1, 8):
        value += from_plane[q]

    total[...] = value
    for peer in column_peers:
        send(total, from_column.at[z], column_sem, peer, 1)
    send_snapshots(1)
    from_column[z] = value
    passed(from_column.at[pl.ds(0, 7)], column_sem)
    for h in range(2):
        value = from_column[h * NZL]
        for i in range(1, NZL):
            value += from_column[h * NZL + i]
        coeffs[core, y, x, h] = value

    for peer in x_peers:
        send(coeffs.at[core, y, x], coeffs.at[core, y, x], x_sem, peer, 2)
    send_snapshots(2)
    send_snapshots(3)
    passed(coeffs.at[0, 0, pl.ds(0, 3)], x_sem)
    for peer in y_peers:
        send(coeffs.at[core, y], coeffs.at[core, y], y_sem, peer, 3)
    passed(coeffs.at[0, pl.ds(0, 3)], y_sem)
    send(coeffs.at[core], coeffs.at[core], core_sem, other_core, 4)
    passed(coeffs.at[0], core_sem)

    rows = [
        coeffs[c_, y_, x_, h]
        for h in range(2) for x_ in range(NX) for y_ in range(NY) for c_ in range(NCORE)
    ]
    whole = jnp.concatenate(rows, axis=0)
    first = lax.broadcasted_iota(jnp.int32, whole.shape, 0) == 0
    energy_load.wait()
    scaled = jnp.where(first, 0.0, pltpu.roll(whole, 1, 0)) * energy_v[...]
    scaled_high, scaled_low = two_parts(scaled)
    weights[...] = (
        dot(vec_t[...], scaled_high, ALONG_LAST) + dot(vec_t[...], scaled_low, ALONG_LAST)
    ).astype(BF16)

    owner_zl = (z + 2) & 3
    side = ((z + 6 - owner_zl) & 7) >> 2
    owner_space = y * 8 + owner_zl * 2 + core
    for c in range(CHUNKS):
        passed(gathered.at[c], snap_sem.at[c])
        rebuilt[c] = dot(weights[...], gathered[c]).astype(BF16)
        start = pl.multiple_of((x * 2 + side) * piece + c * width, width)
        for d in range(8):
            to = tm ^ d
            send(
                rebuilt.at[c, pl.ds(pl.multiple_of(to * hours, hours), hours), :],
                modes.at[:, pl.ds(start, width)],
                modes_sem, (to, owner_space), 5 + CHUNKS,
            )

    whole_high, whole_low = two_parts(whole)
    operator[...] = (
        dot(whole_high, scaled_high, ALONG_FIRST)
        + dot(whole_high, scaled_low, ALONG_FIRST)
        + dot(whole_low, scaled_high, ALONG_FIRST)
    )

    passed(parts.at[pl.ds(0, 7)], sent_sem.at[0])
    passed(from_column.at[pl.ds(0, 7)], sent_sem.at[1])
    passed(coeffs.at[0, 0, pl.ds(0, 3)], sent_sem.at[2])
    passed(coeffs.at[0, pl.ds(0, 3)], sent_sem.at[3])
    passed(coeffs.at[0], sent_sem.at[4])
    for c in range(CHUNKS):
        passed(gathered.at[c], sent_sem.at[5 + c])
    passed(rebuilt, sent_sem.at[5 + CHUNKS])
    passed(modes, modes_sem)


def store_kernel(operator, modes, operator_out, modes_out, sems):
    copies = [
        pltpu.make_async_copy(modes, modes_out, sems.at[0]),
        pltpu.make_async_copy(operator, operator_out, sems.at[1]),
    ]
    for copy in copies:
        copy.start()
    for copy in copies:
        copy.wait()


def per_device(eof_basis, snapshots, inverse_energy, eigen_vectors):
    cells, rank = eof_basis.shape
    hours = snapshots.shape[1]
    all_modes = eigen_vectors.shape[1]
    piece = cells // 8
    width = piece // CHUNKS
    anywhere = pl.BlockSpec(memory_space=pl.ANY)
    on_chip = pl.BlockSpec(memory_space=pltpu.VMEM)
    outputs = pl.pallas_call(
        kernel,
        out_shape=(pltpu.VMEM((rank, rank), F32), pltpu.VMEM((hours, cells), BF16)),
        in_specs=[anywhere] * 4,
        out_specs=(on_chip, on_chip),
        scratch_shapes=[
            pltpu.VMEM((cells, rank), BF16),
            pltpu.VMEM((hours, cells), BF16),
            pltpu.VMEM((rank, all_modes), BF16),
            pltpu.VMEM((all_modes, rank), BF16),
            pltpu.VMEM((8, 8, rank), F32),
            pltpu.VMEM((8, 8, rank), F32),
            pltpu.VMEM((NZ, 8, rank), F32),
            pltpu.VMEM((8, rank), F32),
            pltpu.VMEM((NCORE, NY, NX, 2, 8, rank), F32),
            pltpu.VMEM((CHUNKS, 8 * hours, width), BF16),
            pltpu.VMEM((all_modes, 8 * hours), BF16),
            pltpu.VMEM((CHUNKS, all_modes, width), BF16),
            pltpu.VMEM((1, rank), F32),
            pltpu.SemaphoreType.DMA((3 + K_CHUNKS,)),
            pltpu.SemaphoreType.DMA((6 + CHUNKS,)),
            pltpu.SemaphoreType.DMA,
            pltpu.SemaphoreType.DMA,
            pltpu.SemaphoreType.DMA,
            pltpu.SemaphoreType.DMA,
            pltpu.SemaphoreType.DMA,
            pltpu.SemaphoreType.DMA((CHUNKS,)),
            pltpu.SemaphoreType.DMA,
        ],
        compiler_params=pltpu.CompilerParams(
            collective_id=0, has_side_effects=True, vmem_limit_bytes=60 * 1024 * 1024
        ),
    )(eof_basis, snapshots.T, inverse_energy.reshape(1, rank), eigen_vectors)
    return pl.pallas_call(
        store_kernel,
        out_shape=(
            jax.ShapeDtypeStruct((rank, rank), F32),
            jax.ShapeDtypeStruct((hours, cells), BF16),
        ),
        in_specs=[on_chip, on_chip],
        out_specs=(anywhere, anywhere),
        scratch_shapes=[pltpu.SemaphoreType.DMA((2,))],
    )(*[pltpu.with_memory_space_constraint(a, pltpu.VMEM) for a in outputs])


def solution(mesh):
    in_specs = (P("space", None), P("space", "tm"), P(), P())
    out_specs = (P(), P("tm", "space"))
    return jax.shard_map(
        per_device, mesh=mesh, in_specs=in_specs, out_specs=out_specs, check_vma=False
    )
```

```python
import functools

import jax
import jax.numpy as jnp
from jax import lax
from jax.experimental import pallas as pl
from jax.experimental.pallas import tpu as pltpu
from jax.sharding import PartitionSpec as P

MESH = pl.DeviceIdType.MESH
F32, BF16 = jnp.float32, jnp.bfloat16

NX, NY, NZ, NZL, NCORE = 4, 4, 8, 4, 2
CHUNKS = 4
SAME, CROSS = (0,), (1, 3, 2)
SCHEDULE = (
    ((0, SAME),),
    ((0, CROSS),),
    ((1, SAME), (1, CROSS)),
    ((2, SAME), (3, SAME), (2, CROSS), (3, CROSS)),
)
SAME_MODES, CROSS_MODES = (0, 4), (1, 5, 3, 7, 2, 6)
STORES = 4
K_CHUNKS = 4
EARLY = 2
PRODUCT = (((1,), (0,)), ((), ()))
ALONG_LAST = (((1,), (1,)), ((), ()))
ALONG_FIRST = (((0,), (0,)), ((), ()))


def dot(a, b, dims=PRODUCT):
    return lax.dot_general(a, b, dims, preferred_element_type=F32)


def two_parts(a):
    high = a.astype(BF16)
    return high, (a - high.astype(F32)).astype(BF16)


def kernel(
    eof, snap, energy, vectors, operator, modes,
    eof_v, snap_v, vec_v, vec_t, parts, from_plane, from_column, total, coeffs,
    gathered, weights, rebuilt, energy_v,
    load_sem, sent_sem, word_sem, plane_sem, column_sem, plane_all_sem, core_sem,
    snap_sem, modes_sem,
):
    hours, cells = snap.shape
    piece = cells // 8
    width = piece // CHUNKS
    depth = cells // K_CHUNKS

    def load(source, target, i):
        copy = pltpu.make_async_copy(source, target, load_sem.at[i])
        copy.start()
        return copy

    snap_load = load(snap, snap_v, 0)
    eof_loads = [
        load(eof.at[pl.ds(k * depth, depth), :], eof_v.at[pl.ds(k * depth, depth), :], 1 + k)
        for k in range(K_CHUNKS)
    ]
    vec_load = load(vectors, vec_v, 1 + K_CHUNKS)
    energy_load = load(energy, energy_v, 2 + K_CHUNKS)

    tm, space = lax.axis_index("tm"), lax.axis_index("space")
    zh, x = tm >> 2, tm & 3
    y, zl, core = space >> 3, (space >> 1) & 3, space & 1
    z = zh * NZL + zl

    def at(x_, y_, z_, core_):
        return ((z_ & 4) + x_, y_ * 8 + (z_ & 3) * 2 + core_)

    mine, here = y * 2 + core, y * NX + x
    plane = [mine ^ d for d in range(1, 8)]
    plane_peers = [at(x, q >> 1, z, q & 1) for q in plane]
    column_peers = [at(x, y, z ^ d, core) for d in range(1, NZ)]
    xs = [x ^ d for d in range(NX)]
    x_peers = [at(x_, y, z, core) for x_ in xs[1:]]
    across_peers = [at(x_, y ^ d, z, core) for d in range(1, NY) for x_ in xs]
    other_core = at(x, y, z, core ^ 1)
    far = [(zl + 2) & 7, (zl + 6) & 7]
    far_peers = [[at(x_, y, z_, core) for z_ in far] for x_ in xs]
    beside_peers = [at(x, y, (z + d) & 7, core) for d in (1, 7)]

    def tell(semaphore, peers):
        for peer in peers:
            pl.semaphore_signal(semaphore, inc=1, device_id=peer, device_id_type=MESH)

    barrier = pltpu.get_barrier_semaphore()
    near_peers = far_peers[0] + x_peers + plane_peers + beside_peers
    tell(barrier, near_peers)

    def send(source, target, receive, peer, group):
        pltpu.make_async_remote_copy(
            src_ref=source, dst_ref=target, send_sem=sent_sem.at[group], recv_sem=receive,
            device_id=peer, device_id_type=MESH,
        ).start()

    def passed(ref, sem):
        pltpu.make_async_copy(ref, ref, sem).wait()

    def send_snapshots(point):
        for c, offsets in SCHEDULE[point]:
            for d in offsets:
                for s in range(2):
                    start = pl.multiple_of((xs[d] * 2 + s) * piece + c * width, width)
                    send(
                        snap.at[:, pl.ds(start, width)],
                        gathered.at[c, pl.ds(pl.multiple_of(tm * hours, hours), hours), :],
                        snap_sem.at[c], far_peers[d][s], 4 + c,
                    )

    def project(k):
        eof_loads[k].wait()
        return dot(snap_v[:, k * depth:(k + 1) * depth], eof_v[k * depth:(k + 1) * depth, :])

    snap_load.wait()
    partial = project(0)
    for k in range(1, EARLY):
        partial += project(k)
    pl.semaphore_wait(barrier, len(near_peers))
    tell(word_sem.at[0], x_peers)
    tell(word_sem.at[1], far_peers[0])
    send_snapshots(0)
    for k in range(EARLY, K_CHUNKS):
        partial += project(k)
    for q in range(8):
        parts[q] = partial[q * 8:(q + 1) * 8, :]

    for q, peer in zip(plane, plane_peers):
        send(parts.at[q], from_plane.at[mine], plane_sem, peer, 0)
    pl.semaphore_wait(word_sem.at[0], len(x_peers))
    send_snapshots(1)
    from_plane[mine] = parts[mine]
    vec_load.wait()
    vec_t[...] = vec_v[...].T
    passed(from_plane.at[pl.ds(0, 7)], plane_sem)
    value = from_plane[0]
    for q in range(1, 8):
        value += from_plane[q]

    total[...] = value
    pl.semaphore_wait(word_sem.at[1], 2)
    for peer in column_peers:
        send(total, from_column.at[z], column_sem, peer, 1)
    send_snapshots(2)
    from_column[z] = value
    passed(from_column.at[pl.ds(0, 7)], column_sem)
    for h in range(2):
        value = from_column[h * NZL]
        for i in range(1, NZL):
            value += from_column[h * NZL + i]
        coeffs[core, here, h] = value

    for peer in across_peers + x_peers:
        send(coeffs.at[core, here], coeffs.at[core, here], plane_all_sem, peer, 2)
    send_snapshots(3)
    passed(coeffs.at[0, pl.ds(0, 15)], plane_all_sem)
    send(coeffs.at[core], coeffs.at[core], core_sem, other_core, 3)
    passed(coeffs.at[0], core_sem)

    rows = [
        coeffs[c_, y_ * NX + x_, h]
        for h in range(2) for x_ in range(NX) for y_ in range(NY) for c_ in range(NCORE)
    ]
    whole = jnp.concatenate(rows, axis=0)
    first = lax.broadcasted_iota(jnp.int32, whole.shape, 0) == 0
    energy_load.wait()
    scaled = jnp.where(first, 0.0, pltpu.roll(whole, 1, 0)) * energy_v[...]
    scaled_high, scaled_low = two_parts(scaled)
    weights[...] = (
        dot(vec_t[...], scaled_high, ALONG_LAST) + dot(vec_t[...], scaled_low, ALONG_LAST)
    ).astype(BF16)

    owner_zl = (z + 2) & 3
    side = ((z + 6 - owner_zl) & 7) >> 2
    owner_space = y * 8 + owner_zl * 2 + core
    def send_modes(c, offsets, group):
        start = pl.multiple_of((x * 2 + side) * piece + c * width, width)
        for d in offsets:
            to = tm ^ d
            send(
                rebuilt.at[c, pl.ds(pl.multiple_of(to * hours, hours), hours), :],
                modes.at[:, pl.ds(start, width)],
                modes_sem, (to, owner_space), group,
            )

    for c in range(CHUNKS):
        passed(gathered.at[c], snap_sem.at[c])
        rebuilt[c] = dot(weights[...], gathered[c]).astype(BF16)
        send_modes(c, CROSS_MODES, 4 + CHUNKS + c)

    whole_high, whole_low = two_parts(whole)
    operator[...] = (
        dot(whole_high, scaled_high, ALONG_FIRST)
        + dot(whole_high, scaled_low, ALONG_FIRST)
        + dot(whole_low, scaled_high, ALONG_FIRST)
    )

    for c in range(CHUNKS):
        passed(rebuilt.at[c, pl.ds(0, 6 * hours)], sent_sem.at[4 + CHUNKS + c])
        send_modes(c, SAME_MODES, 4 + 2 * CHUNKS)

    passed(parts.at[pl.ds(0, 7)], sent_sem.at[0])
    passed(from_column.at[pl.ds(0, 7)], sent_sem.at[1])
    passed(coeffs.at[0, pl.ds(0, 15)], sent_sem.at[2])
    passed(coeffs.at[0], sent_sem.at[3])
    for c in range(CHUNKS):
        passed(gathered.at[c], sent_sem.at[4 + c])
    passed(rebuilt.at[:, pl.ds(0, 2 * hours)], sent_sem.at[4 + 2 * CHUNKS])
    passed(modes, modes_sem)


def store_kernel(operator, modes, operator_out, modes_out, sems):
    step = modes.shape[1] // STORES
    copies = [
        pltpu.make_async_copy(modes.at[:, pl.ds(i * step, step)], modes_out.at[:, pl.ds(i * step, step)], sems.at[i])
        for i in range(STORES)
    ]
    copies.append(pltpu.make_async_copy(operator, operator_out, sems.at[STORES]))
    for copy in copies:
        copy.start()
    for copy in copies:
        copy.wait()


def per_device(eof_basis, snapshots, inverse_energy, eigen_vectors):
    cells, rank = eof_basis.shape
    hours = snapshots.shape[1]
    all_modes = eigen_vectors.shape[1]
    piece = cells // 8
    width = piece // CHUNKS
    anywhere = pl.BlockSpec(memory_space=pl.ANY)
    on_chip = pl.BlockSpec(memory_space=pltpu.VMEM)
    outputs = pl.pallas_call(
        kernel,
        out_shape=(pltpu.VMEM((rank, rank), F32), pltpu.VMEM((hours, cells), BF16)),
        in_specs=[anywhere] * 4,
        out_specs=(on_chip, on_chip),
        scratch_shapes=[
            pltpu.VMEM((cells, rank), BF16),
            pltpu.VMEM((hours, cells), BF16),
            pltpu.VMEM((rank, all_modes), BF16),
            pltpu.VMEM((all_modes, rank), BF16),
            pltpu.VMEM((8, 8, rank), F32),
            pltpu.VMEM((8, 8, rank), F32),
            pltpu.VMEM((NZ, 8, rank), F32),
            pltpu.VMEM((8, rank), F32),
            pltpu.VMEM((NCORE, NY * NX, 2, 8, rank), F32),
            pltpu.VMEM((CHUNKS, 8 * hours, width), BF16),
            pltpu.VMEM((all_modes, 8 * hours), BF16),
            pltpu.VMEM((CHUNKS, all_modes, width), BF16),
            pltpu.VMEM((1, rank), F32),
            pltpu.SemaphoreType.DMA((3 + K_CHUNKS,)),
            pltpu.SemaphoreType.DMA((5 + 2 * CHUNKS,)),
            pltpu.SemaphoreType.REGULAR((2,)),
            pltpu.SemaphoreType.DMA,
            pltpu.SemaphoreType.DMA,
            pltpu.SemaphoreType.DMA,
            pltpu.SemaphoreType.DMA,
            pltpu.SemaphoreType.DMA((CHUNKS,)),
            pltpu.SemaphoreType.DMA,
        ],
        compiler_params=pltpu.CompilerParams(
            collective_id=0, has_side_effects=True, vmem_limit_bytes=60 * 1024 * 1024
        ),
    )(eof_basis, snapshots.T, inverse_energy.reshape(1, rank), eigen_vectors)
    return pl.pallas_call(
        store_kernel,
        out_shape=(
            jax.ShapeDtypeStruct((rank, rank), F32),
            jax.ShapeDtypeStruct((hours, cells), BF16),
        ),
        in_specs=[on_chip, on_chip],
        out_specs=(anywhere, anywhere),
        scratch_shapes=[pltpu.SemaphoreType.DMA((STORES + 1,))],
    )(*[pltpu.with_memory_space_constraint(a, pltpu.VMEM) for a in outputs])


def solution(mesh):
    in_specs = (P("space", None), P("space", "tm"), P(), P())
    out_specs = (P(), P("tm", "space"))
    return jax.shard_map(
        per_device, mesh=mesh, in_specs=in_specs, out_specs=out_specs, check_vma=False
    )
```

```python
import functools

import jax
import jax.numpy as jnp
from jax import lax
from jax.experimental import pallas as pl
from jax.experimental.pallas import tpu as pltpu
from jax.sharding import PartitionSpec as P

MESH = pl.DeviceIdType.MESH
F32, BF16 = jnp.float32, jnp.bfloat16

NX, NY, NZ, NZL, NCORE = 4, 4, 8, 4, 2
CHUNKS = 4
SAME, CROSS = (0,), (1, 3, 2)
SCHEDULE = (
    ((0, SAME),),
    ((0, CROSS), (1, SAME)),
    ((1, CROSS), (2, SAME)),
    ((3, SAME), (2, CROSS), (3, CROSS)),
)
SAME_MODES, CROSS_MODES = (0, 4), (1, 5, 3, 7, 2, 6)
STORES = 4
K_CHUNKS = 4
EARLY = 2
PRODUCT = (((1,), (0,)), ((), ()))
ALONG_LAST = (((1,), (1,)), ((), ()))
ALONG_FIRST = (((0,), (0,)), ((), ()))


def dot(a, b, dims=PRODUCT):
    return lax.dot_general(a, b, dims, preferred_element_type=F32)


def two_parts(a):
    high = a.astype(BF16)
    return high, (a - high.astype(F32)).astype(BF16)


def kernel(
    eof, snap, energy, vectors, operator, modes,
    eof_v, snap_v, vec_v, vec_t, parts, from_plane, from_column, total, coeffs,
    gathered, weights, rebuilt, energy_v,
    load_sem, sent_sem, word_sem, plane_sem, column_sem, plane_all_sem, core_sem,
    snap_sem, modes_sem,
):
    hours, cells = snap.shape
    piece = cells // 8
    width = piece // CHUNKS
    depth = cells // K_CHUNKS

    def load(source, target, i):
        copy = pltpu.make_async_copy(source, target, load_sem.at[i])
        copy.start()
        return copy

    snap_load = load(snap, snap_v, 0)
    eof_loads = [
        load(eof.at[pl.ds(k * depth, depth), :], eof_v.at[pl.ds(k * depth, depth), :], 1 + k)
        for k in range(K_CHUNKS)
    ]
    vec_load = load(vectors, vec_v, 1 + K_CHUNKS)
    energy_load = load(energy, energy_v, 2 + K_CHUNKS)

    tm, space = lax.axis_index("tm"), lax.axis_index("space")
    zh, x = tm >> 2, tm & 3
    y, zl, core = space >> 3, (space >> 1) & 3, space & 1
    z = zh * NZL + zl

    def at(x_, y_, z_, core_):
        return ((z_ & 4) + x_, y_ * 8 + (z_ & 3) * 2 + core_)

    mine, here = y * 2 + core, y * NX + x
    plane = [mine ^ d for d in range(1, 8)]
    plane_peers = [at(x, q >> 1, z, q & 1) for q in plane]
    column_peers = [at(x, y, z ^ d, core) for d in range(1, NZ)]
    xs = [x ^ d for d in range(NX)]
    x_peers = [at(x_, y, z, core) for x_ in xs[1:]]
    across_peers = [at(x_, y ^ d, z, core) for d in range(1, NY) for x_ in xs]
    other_core = at(x, y, z, core ^ 1)
    far = [(zl + 2) & 7, (zl + 6) & 7]
    far_peers = [[at(x_, y, z_, core) for z_ in far] for x_ in xs]
    beside_peers = [at(x, y, (z + d) & 7, core) for d in (1, 7)]

    def tell(semaphore, peers):
        for peer in peers:
            pl.semaphore_signal(semaphore, inc=1, device_id=peer, device_id_type=MESH)

    barrier = pltpu.get_barrier_semaphore()
    near_peers = far_peers[0] + x_peers + plane_peers + beside_peers
    tell(barrier, near_peers)

    def send(source, target, receive, peer, group):
        pltpu.make_async_remote_copy(
            src_ref=source, dst_ref=target, send_sem=sent_sem.at[group], recv_sem=receive,
            device_id=peer, device_id_type=MESH,
        ).start()

    def passed(ref, sem):
        pltpu.make_async_copy(ref, ref, sem).wait()

    def send_snapshots(point):
        for c, offsets in SCHEDULE[point]:
            for d in offsets:
                for s in range(2):
                    start = pl.multiple_of((xs[d] * 2 + s) * piece + c * width, width)
                    send(
                        snap_v.at[:, pl.ds(start, width)],
                        gathered.at[c, pl.ds(pl.multiple_of(tm * hours, hours), hours), :],
                        snap_sem.at[c], far_peers[d][s], 4 + c,
                    )

    def project(k):
        eof_loads[k].wait()
        return dot(snap_v[:, k * depth:(k + 1) * depth], eof_v[k * depth:(k + 1) * depth, :])

    snap_load.wait()
    partial = project(0)
    for k in range(1, EARLY):
        partial += project(k)
    pl.semaphore_wait(barrier, len(near_peers))
    tell(word_sem.at[0], x_peers)
    tell(word_sem.at[1], far_peers[0])
    send_snapshots(0)
    for k in range(EARLY, K_CHUNKS):
        partial += project(k)
    for q in range(8):
        parts[q] = partial[q * 8:(q + 1) * 8, :]

    for q, peer in zip(plane, plane_peers):
        send(parts.at[q], from_plane.at[mine], plane_sem, peer, 0)
    pl.semaphore_wait(word_sem.at[0], len(x_peers))
    send_snapshots(1)
    from_plane[mine] = parts[mine]
    vec_load.wait()
    vec_t[...] = vec_v[...].T
    passed(from_plane.at[pl.ds(0, 7)], plane_sem)
    value = from_plane[0]
    for q in range(1, 8):
        value += from_plane[q]

    total[...] = value
    pl.semaphore_wait(word_sem.at[1], 2)
    for peer in column_peers:
        send(total, from_column.at[z], column_sem, peer, 1)
    send_snapshots(2)
    from_column[z] = value
    passed(from_column.at[pl.ds(0, 7)], column_sem)
    for h in range(2):
        value = from_column[h * NZL]
        for i in range(1, NZL):
            value += from_column[h * NZL + i]
        coeffs[core, here, h] = value

    for peer in across_peers + x_peers:
        send(coeffs.at[core, here], coeffs.at[core, here], plane_all_sem, peer, 2)
    send_snapshots(3)
    passed(coeffs.at[0, pl.ds(0, 15)], plane_all_sem)
    send(coeffs.at[core], coeffs.at[core], core_sem, other_core, 3)
    passed(coeffs.at[0], core_sem)

    rows = [
        coeffs[c_, y_ * NX + x_, h]
        for h in range(2) for x_ in range(NX) for y_ in range(NY) for c_ in range(NCORE)
    ]
    whole = jnp.concatenate(rows, axis=0)
    first = lax.broadcasted_iota(jnp.int32, whole.shape, 0) == 0
    energy_load.wait()
    scaled = jnp.where(first, 0.0, pltpu.roll(whole, 1, 0)) * energy_v[...]
    scaled_high, scaled_low = two_parts(scaled)
    weights[...] = (
        dot(vec_t[...], scaled_high, ALONG_LAST) + dot(vec_t[...], scaled_low, ALONG_LAST)
    ).astype(BF16)

    owner_zl = (z + 2) & 3
    side = ((z + 6 - owner_zl) & 7) >> 2
    owner_space = y * 8 + owner_zl * 2 + core
    def send_modes(c, offsets, group):
        start = pl.multiple_of((x * 2 + side) * piece + c * width, width)
        for d in offsets:
            to = tm ^ d
            send(
                rebuilt.at[c, pl.ds(pl.multiple_of(to * hours, hours), hours), :],
                modes.at[:, pl.ds(start, width)],
                modes_sem, (to, owner_space), group,
            )

    for c in range(CHUNKS):
        passed(gathered.at[c], snap_sem.at[c])
        rebuilt[c] = dot(weights[...], gathered[c]).astype(BF16)
        send_modes(c, CROSS_MODES, 4 + CHUNKS + c)

    whole_high, whole_low = two_parts(whole)
    operator[...] = (
        dot(whole_high, scaled_high, ALONG_FIRST)
        + dot(whole_high, scaled_low, ALONG_FIRST)
        + dot(whole_low, scaled_high, ALONG_FIRST)
    )

    for c in range(CHUNKS):
        passed(rebuilt.at[c, pl.ds(0, 6 * hours)], sent_sem.at[4 + CHUNKS + c])
        send_modes(c, SAME_MODES, 4 + 2 * CHUNKS)

    passed(parts.at[pl.ds(0, 7)], sent_sem.at[0])
    passed(from_column.at[pl.ds(0, 7)], sent_sem.at[1])
    passed(coeffs.at[0, pl.ds(0, 15)], sent_sem.at[2])
    passed(coeffs.at[0], sent_sem.at[3])
    for c in range(CHUNKS):
        passed(gathered.at[c], sent_sem.at[4 + c])
    passed(rebuilt.at[:, pl.ds(0, 2 * hours)], sent_sem.at[4 + 2 * CHUNKS])
    passed(modes, modes_sem)


def store_kernel(operator, modes, operator_out, modes_out, sems):
    step = modes.shape[1] // STORES
    copies = [
        pltpu.make_async_copy(modes.at[:, pl.ds(i * step, step)], modes_out.at[:, pl.ds(i * step, step)], sems.at[i])
        for i in range(STORES)
    ]
    copies.append(pltpu.make_async_copy(operator, operator_out, sems.at[STORES]))
    for copy in copies:
        copy.start()
    for copy in copies:
        copy.wait()


def per_device(eof_basis, snapshots, inverse_energy, eigen_vectors):
    cells, rank = eof_basis.shape
    hours = snapshots.shape[1]
    all_modes = eigen_vectors.shape[1]
    piece = cells // 8
    width = piece // CHUNKS
    anywhere = pl.BlockSpec(memory_space=pl.ANY)
    on_chip = pl.BlockSpec(memory_space=pltpu.VMEM)
    outputs = pl.pallas_call(
        kernel,
        out_shape=(pltpu.VMEM((rank, rank), F32), pltpu.VMEM((hours, cells), BF16)),
        in_specs=[anywhere] * 4,
        out_specs=(on_chip, on_chip),
        scratch_shapes=[
            pltpu.VMEM((cells, rank), BF16),
            pltpu.VMEM((hours, cells), BF16),
            pltpu.VMEM((rank, all_modes), BF16),
            pltpu.VMEM((all_modes, rank), BF16),
            pltpu.VMEM((8, 8, rank), F32),
            pltpu.VMEM((8, 8, rank), F32),
            pltpu.VMEM((NZ, 8, rank), F32),
            pltpu.VMEM((8, rank), F32),
            pltpu.VMEM((NCORE, NY * NX, 2, 8, rank), F32),
            pltpu.VMEM((CHUNKS, 8 * hours, width), BF16),
            pltpu.VMEM((all_modes, 8 * hours), BF16),
            pltpu.VMEM((CHUNKS, all_modes, width), BF16),
            pltpu.VMEM((1, rank), F32),
            pltpu.SemaphoreType.DMA((3 + K_CHUNKS,)),
            pltpu.SemaphoreType.DMA((5 + 2 * CHUNKS,)),
            pltpu.SemaphoreType.REGULAR((2,)),
            pltpu.SemaphoreType.DMA,
            pltpu.SemaphoreType.DMA,
            pltpu.SemaphoreType.DMA,
            pltpu.SemaphoreType.DMA,
            pltpu.SemaphoreType.DMA((CHUNKS,)),
            pltpu.SemaphoreType.DMA,
        ],
        compiler_params=pltpu.CompilerParams(
            collective_id=0, has_side_effects=True, vmem_limit_bytes=60 * 1024 * 1024
        ),
    )(eof_basis, snapshots.T, inverse_energy.reshape(1, rank), eigen_vectors)
    return pl.pallas_call(
        store_kernel,
        out_shape=(
            jax.ShapeDtypeStruct((rank, rank), F32),
            jax.ShapeDtypeStruct((hours, cells), BF16),
        ),
        in_specs=[on_chip, on_chip],
        out_specs=(anywhere, anywhere),
        scratch_shapes=[pltpu.SemaphoreType.DMA((STORES + 1,))],
    )(*[pltpu.with_memory_space_constraint(a, pltpu.VMEM) for a in outputs])


def solution(mesh):
    in_specs = (P("space", None), P("space", "tm"), P(), P())
    out_specs = (P(), P("tm", "space"))
    return jax.shard_map(
        per_device, mesh=mesh, in_specs=in_specs, out_specs=out_specs, check_vma=False
    )
```

```python
import functools

import jax
import jax.numpy as jnp
from jax import lax
from jax.experimental import pallas as pl
from jax.experimental.pallas import tpu as pltpu
from jax.sharding import PartitionSpec as P

MESH = pl.DeviceIdType.MESH
F32, BF16 = jnp.float32, jnp.bfloat16

NX, NY, NZ, NZL, NCORE = 4, 4, 8, 4, 2
CHUNKS = 4
SAME, CROSS = (0,), (1, 3, 2)
SCHEDULE = (
    ((0, SAME),),
    ((0, CROSS), (1, SAME)),
    ((1, CROSS), (2, SAME)),
    ((3, SAME), (2, CROSS), (3, CROSS)),
)
SAME_MODES, CROSS_MODES = (0, 4), (1, 5, 3, 7, 2, 6)
STORES = 4
K_CHUNKS = 4
EARLY = 2
PRODUCT = (((1,), (0,)), ((), ()))
ALONG_LAST = (((1,), (1,)), ((), ()))
ALONG_FIRST = (((0,), (0,)), ((), ()))


def dot(a, b, dims=PRODUCT):
    return lax.dot_general(a, b, dims, preferred_element_type=F32)


def two_parts(a):
    high = a.astype(BF16)
    return high, (a - high.astype(F32)).astype(BF16)


def kernel(
    eof, snap, energy, vectors, operator, modes,
    eof_v, snap_v, vec_v, vec_t, parts, from_plane, from_column, total, coeffs,
    gathered, weights, rebuilt, energy_v,
    load_sem, sent_sem, word_sem, plane_sem, column_sem, plane_all_sem, core_sem,
    snap_sem, modes_sem,
):
    hours, cells = snap.shape
    piece = cells // 8
    width = piece // CHUNKS
    depth = cells // K_CHUNKS

    def load(source, target, i):
        copy = pltpu.make_async_copy(source, target, load_sem.at[i])
        copy.start()
        return copy

    snap_load = load(snap, snap_v, 0)
    eof_loads = [
        load(eof.at[pl.ds(k * depth, depth), :], eof_v.at[pl.ds(k * depth, depth), :], 1 + k)
        for k in range(K_CHUNKS)
    ]
    vec_load = load(vectors, vec_v, 1 + K_CHUNKS)
    energy_load = load(energy, energy_v, 2 + K_CHUNKS)

    tm, space = lax.axis_index("tm"), lax.axis_index("space")
    zh, x = tm >> 2, tm & 3
    y, zl, core = space >> 3, (space >> 1) & 3, space & 1
    z = zh * NZL + zl

    def at(x_, y_, z_, core_):
        return ((z_ & 4) + x_, y_ * 8 + (z_ & 3) * 2 + core_)

    mine, here = y * 2 + core, y * NX + x
    plane = [mine ^ d for d in range(1, 8)]
    plane_peers = [at(x, q >> 1, z, q & 1) for q in plane]
    column_peers = [at(x, y, z ^ d, core) for d in (4, 5, 3, 7, 2, 6, 1)]
    xs = [x ^ d for d in range(NX)]
    x_peers = [at(x_, y, z, core) for x_ in xs[1:]]
    across_peers = [at(x_, y ^ d, z, core) for d in range(1, NY) for x_ in xs]
    other_core = at(x, y, z, core ^ 1)
    far = [(zl + 2) & 7, (zl + 6) & 7]
    far_peers = [[at(x_, y, z_, core) for z_ in far] for x_ in xs]
    beside_peers = [at(x, y, (z + d) & 7, core) for d in (1, 7)]

    def tell(semaphore, peers):
        for peer in peers:
            pl.semaphore_signal(semaphore, inc=1, device_id=peer, device_id_type=MESH)

    barrier = pltpu.get_barrier_semaphore()
    near_peers = far_peers[0] + x_peers + plane_peers + beside_peers
    tell(barrier, near_peers)

    def send(source, target, receive, peer, group):
        pltpu.make_async_remote_copy(
            src_ref=source, dst_ref=target, send_sem=sent_sem.at[group], recv_sem=receive,
            device_id=peer, device_id_type=MESH,
        ).start()

    def passed(ref, sem):
        pltpu.make_async_copy(ref, ref, sem).wait()

    def send_snapshots(point):
        for c, offsets in SCHEDULE[point]:
            for d in offsets:
                for s in range(2):
                    start = pl.multiple_of((xs[d] * 2 + s) * piece + c * width, width)
                    send(
                        snap_v.at[:, pl.ds(start, width)],
                        gathered.at[c, pl.ds(pl.multiple_of(tm * hours, hours), hours), :],
                        snap_sem.at[c], far_peers[d][s], 4 + c,
                    )

    def project(k):
        eof_loads[k].wait()
        return dot(snap_v[:, k * depth:(k + 1) * depth], eof_v[k * depth:(k + 1) * depth, :])

    snap_load.wait()
    partial = project(0)
    for k in range(1, EARLY):
        partial += project(k)
    pl.semaphore_wait(barrier, len(near_peers))
    tell(word_sem.at[0], x_peers)
    tell(word_sem.at[1], far_peers[0])
    send_snapshots(0)
    for k in range(EARLY, K_CHUNKS):
        partial += project(k)
    for q in range(8):
        parts[q] = partial[q * 8:(q + 1) * 8, :]

    for q, peer in zip(plane, plane_peers):
        send(parts.at[q], from_plane.at[mine], plane_sem, peer, 0)
    pl.semaphore_wait(word_sem.at[0], len(x_peers))
    send_snapshots(1)
    from_plane[mine] = parts[mine]
    vec_load.wait()
    vec_t[...] = vec_v[...].T
    passed(from_plane.at[pl.ds(0, 7)], plane_sem)
    value = from_plane[0]
    for q in range(1, 8):
        value += from_plane[q]

    total[...] = value
    pl.semaphore_wait(word_sem.at[1], 2)
    for peer in column_peers:
        send(total, from_column.at[z], column_sem, peer, 1)
    send_snapshots(2)
    from_column[z] = value
    passed(from_column.at[pl.ds(0, 7)], column_sem)
    for h in range(2):
        value = from_column[h * NZL]
        for i in range(1, NZL):
            value += from_column[h * NZL + i]
        coeffs[core, here, h] = value

    for peer in across_peers + x_peers:
        send(coeffs.at[core, here], coeffs.at[core, here], plane_all_sem, peer, 2)
    send_snapshots(3)
    passed(coeffs.at[0, pl.ds(0, 15)], plane_all_sem)
    send(coeffs.at[core], coeffs.at[core], core_sem, other_core, 3)
    passed(coeffs.at[0], core_sem)

    rows = [
        coeffs[c_, y_ * NX + x_, h]
        for h in range(2) for x_ in range(NX) for y_ in range(NY) for c_ in range(NCORE)
    ]
    whole = jnp.concatenate(rows, axis=0)
    first = lax.broadcasted_iota(jnp.int32, whole.shape, 0) == 0
    energy_load.wait()
    scaled = jnp.where(first, 0.0, pltpu.roll(whole, 1, 0)) * energy_v[...]
    scaled_high, scaled_low = two_parts(scaled)
    weights[...] = (
        dot(vec_t[...], scaled_high, ALONG_LAST) + dot(vec_t[...], scaled_low, ALONG_LAST)
    ).astype(BF16)

    owner_zl = (z + 2) & 3
    side = ((z + 6 - owner_zl) & 7) >> 2
    owner_space = y * 8 + owner_zl * 2 + core

    def send_modes(c, offsets, group):
        start = pl.multiple_of((x * 2 + side) * piece + c * width, width)
        for d in offsets:
            to = tm ^ d
            send(
                rebuilt.at[c, pl.ds(pl.multiple_of(to * hours, hours), hours), :],
                modes.at[:, pl.ds(start, width)],
                modes_sem, (to, owner_space), group,
            )

    for c in range(CHUNKS):
        passed(gathered.at[c], snap_sem.at[c])
        rebuilt[c] = dot(weights[...], gathered[c]).astype(BF16)
        send_modes(c, CROSS_MODES, 4 + CHUNKS + c)

    whole_high, whole_low = two_parts(whole)
    operator[...] = (
        dot(whole_high, scaled_high, ALONG_FIRST)
        + dot(whole_high, scaled_low, ALONG_FIRST)
        + dot(whole_low, scaled_high, ALONG_FIRST)
    )

    for c in range(CHUNKS):
        passed(rebuilt.at[c, pl.ds(0, 6 * hours)], sent_sem.at[4 + CHUNKS + c])
        send_modes(c, SAME_MODES, 4 + 2 * CHUNKS)

    passed(parts.at[pl.ds(0, 7)], sent_sem.at[0])
    passed(from_column.at[pl.ds(0, 7)], sent_sem.at[1])
    passed(coeffs.at[0, pl.ds(0, 15)], sent_sem.at[2])
    passed(coeffs.at[0], sent_sem.at[3])
    for c in range(CHUNKS):
        passed(gathered.at[c], sent_sem.at[4 + c])
    passed(rebuilt.at[:, pl.ds(0, 2 * hours)], sent_sem.at[4 + 2 * CHUNKS])
    passed(modes, modes_sem)


def store_kernel(operator, modes, operator_out, modes_out, sems):
    step = modes.shape[1] // STORES
    copies = [
        pltpu.make_async_copy(modes.at[:, pl.ds(i * step, step)], modes_out.at[:, pl.ds(i * step, step)], sems.at[i])
        for i in range(STORES)
    ]
    copies.append(pltpu.make_async_copy(operator, operator_out, sems.at[STORES]))
    for copy in copies:
        copy.start()
    for copy in copies:
        copy.wait()


def per_device(eof_basis, snapshots, inverse_energy, eigen_vectors):
    cells, rank = eof_basis.shape
    hours = snapshots.shape[1]
    all_modes = eigen_vectors.shape[1]
    piece = cells // 8
    width = piece // CHUNKS
    anywhere = pl.BlockSpec(memory_space=pl.ANY)
    on_chip = pl.BlockSpec(memory_space=pltpu.VMEM)
    outputs = pl.pallas_call(
        kernel,
        out_shape=(pltpu.VMEM((rank, rank), F32), pltpu.VMEM((hours, cells), BF16)),
        in_specs=[anywhere] * 4,
        out_specs=(on_chip, on_chip),
        scratch_shapes=[
            pltpu.VMEM((cells, rank), BF16),
            pltpu.VMEM((hours, cells), BF16),
            pltpu.VMEM((rank, all_modes), BF16),
            pltpu.VMEM((all_modes, rank), BF16),
            pltpu.VMEM((8, 8, rank), F32),
            pltpu.VMEM((8, 8, rank), F32),
            pltpu.VMEM((NZ, 8, rank), F32),
            pltpu.VMEM((8, rank), F32),
            pltpu.VMEM((NCORE, NY * NX, 2, 8, rank), F32),
            pltpu.VMEM((CHUNKS, 8 * hours, width), BF16),
            pltpu.VMEM((all_modes, 8 * hours), BF16),
            pltpu.VMEM((CHUNKS, all_modes, width), BF16),
            pltpu.VMEM((1, rank), F32),
            pltpu.SemaphoreType.DMA((3 + K_CHUNKS,)),
            pltpu.SemaphoreType.DMA((5 + 2 * CHUNKS,)),
            pltpu.SemaphoreType.REGULAR((2,)),
            pltpu.SemaphoreType.DMA,
            pltpu.SemaphoreType.DMA,
            pltpu.SemaphoreType.DMA,
            pltpu.SemaphoreType.DMA,
            pltpu.SemaphoreType.DMA((CHUNKS,)),
            pltpu.SemaphoreType.DMA,
        ],
        compiler_params=pltpu.CompilerParams(
            collective_id=0, has_side_effects=True, vmem_limit_bytes=60 * 1024 * 1024
        ),
    )(eof_basis, snapshots.T, inverse_energy.reshape(1, rank), eigen_vectors)
    return pl.pallas_call(
        store_kernel,
        out_shape=(
            jax.ShapeDtypeStruct((rank, rank), F32),
            jax.ShapeDtypeStruct((hours, cells), BF16),
        ),
        in_specs=[on_chip, on_chip],
        out_specs=(anywhere, anywhere),
        scratch_shapes=[pltpu.SemaphoreType.DMA((STORES + 1,))],
    )(*[pltpu.with_memory_space_constraint(a, pltpu.VMEM) for a in outputs])


def solution(mesh):
    in_specs = (P("space", None), P("space", "tm"), P(), P())
    out_specs = (P(), P("tm", "space"))
    return jax.shard_map(
        per_device, mesh=mesh, in_specs=in_specs, out_specs=out_specs, check_vma=False
    )
```

```python
import functools

import jax
import jax.numpy as jnp
from jax import lax
from jax.experimental import pallas as pl
from jax.experimental.pallas import tpu as pltpu
from jax.sharding import PartitionSpec as P

MESH = pl.DeviceIdType.MESH
F32, BF16 = jnp.float32, jnp.bfloat16

NX, NY, NZ, NZL, NCORE = 4, 4, 8, 4, 2
CHUNKS = 4
SAME, CROSS = (0,), (1, 3, 2)
SCHEDULE = (
    ((0, SAME),),
    ((0, CROSS), (1, SAME)),
    ((1, CROSS),),
    ((2, CROSS), (3, CROSS)),
    ((2, SAME), (3, SAME)),
)
SAME_MODES, CROSS_MODES = (0, 4), (1, 5, 3, 7, 2, 6)
STORES = 4
K_CHUNKS = 4
EARLY = 2
PRODUCT = (((1,), (0,)), ((), ()))
ALONG_LAST = (((1,), (1,)), ((), ()))
ALONG_FIRST = (((0,), (0,)), ((), ()))


def dot(a, b, dims=PRODUCT):
    return lax.dot_general(a, b, dims, preferred_element_type=F32)


def two_parts(a):
    high = a.astype(BF16)
    return high, (a - high.astype(F32)).astype(BF16)


def kernel(
    eof, snap, energy, vectors, operator, modes,
    eof_v, snap_v, vec_v, vec_t, parts, from_plane, from_column, total, coeffs,
    gathered, weights, rebuilt, energy_v,
    load_sem, sent_sem, word_sem, plane_sem, column_sem, plane_all_sem, core_sem,
    snap_sem, modes_sem,
):
    hours, cells = snap.shape
    piece = cells // 8
    width = piece // CHUNKS
    depth = cells // K_CHUNKS

    def load(source, target, i):
        copy = pltpu.make_async_copy(source, target, load_sem.at[i])
        copy.start()
        return copy

    snap_load = load(snap, snap_v, 0)
    eof_loads = [
        load(eof.at[pl.ds(k * depth, depth), :], eof_v.at[pl.ds(k * depth, depth), :], 1 + k)
        for k in range(K_CHUNKS)
    ]
    vec_load = load(vectors, vec_v, 1 + K_CHUNKS)
    energy_load = load(energy, energy_v, 2 + K_CHUNKS)

    tm, space = lax.axis_index("tm"), lax.axis_index("space")
    zh, x = tm >> 2, tm & 3
    y, zl, core = space >> 3, (space >> 1) & 3, space & 1
    z = zh * NZL + zl

    def at(x_, y_, z_, core_):
        return ((z_ & 4) + x_, y_ * 8 + (z_ & 3) * 2 + core_)

    mine, here = y * 2 + core, y * NX + x
    plane = [mine ^ d for d in range(1, 8)]
    plane_peers = [at(x, q >> 1, z, q & 1) for q in plane]
    column_peers = [at(x, y, z ^ d, core) for d in (4, 5, 3, 7, 2, 6, 1)]
    xs = [x ^ d for d in range(NX)]
    x_peers = [at(x_, y, z, core) for x_ in xs[1:]]
    across_peers = [at(x_, y ^ d, z, core) for d in range(1, NY) for x_ in xs]
    other_core = at(x, y, z, core ^ 1)
    far = [(zl + 2) & 7, (zl + 6) & 7]
    far_peers = [[at(x_, y, z_, core) for z_ in far] for x_ in xs]
    beside_peers = [at(x, y, (z + d) & 7, core) for d in (1, 7)]

    def tell(semaphore, peers):
        for peer in peers:
            pl.semaphore_signal(semaphore, inc=1, device_id=peer, device_id_type=MESH)

    barrier = pltpu.get_barrier_semaphore()
    near_peers = far_peers[0] + x_peers + plane_peers + beside_peers
    tell(barrier, near_peers)

    def send(source, target, receive, peer, group):
        pltpu.make_async_remote_copy(
            src_ref=source, dst_ref=target, send_sem=sent_sem.at[group], recv_sem=receive,
            device_id=peer, device_id_type=MESH,
        ).start()

    def passed(ref, sem):
        pltpu.make_async_copy(ref, ref, sem).wait()

    def send_snapshots(point):
        for c, offsets in SCHEDULE[point]:
            for d in offsets:
                for s in range(2):
                    start = pl.multiple_of((xs[d] * 2 + s) * piece + c * width, width)
                    send(
                        snap_v.at[:, pl.ds(start, width)],
                        gathered.at[c, pl.ds(pl.multiple_of(tm * hours, hours), hours), :],
                        snap_sem.at[c], far_peers[d][s], 4 + c,
                    )

    def project(k):
        eof_loads[k].wait()
        return dot(snap_v[:, k * depth:(k + 1) * depth], eof_v[k * depth:(k + 1) * depth, :])

    snap_load.wait()
    partial = project(0)
    for k in range(1, EARLY):
        partial += project(k)
    pl.semaphore_wait(barrier, len(near_peers))
    tell(word_sem.at[0], x_peers)
    tell(word_sem.at[1], far_peers[0])
    send_snapshots(0)
    for k in range(EARLY, K_CHUNKS):
        partial += project(k)
    for q in range(8):
        parts[q] = partial[q * 8:(q + 1) * 8, :]

    for q, peer in zip(plane, plane_peers):
        send(parts.at[q], from_plane.at[mine], plane_sem, peer, 0)
    pl.semaphore_wait(word_sem.at[0], len(x_peers))
    send_snapshots(1)
    from_plane[mine] = parts[mine]
    vec_load.wait()
    vec_t[...] = vec_v[...].T
    passed(from_plane.at[pl.ds(0, 7)], plane_sem)
    value = from_plane[0]
    for q in range(1, 8):
        value += from_plane[q]

    total[...] = value
    pl.semaphore_wait(word_sem.at[1], 2)
    for peer in column_peers:
        send(total, from_column.at[z], column_sem, peer, 1)
    send_snapshots(2)
    from_column[z] = value
    passed(gathered.at[0], sent_sem.at[4])
    send_snapshots(4)
    passed(from_column.at[pl.ds(0, 7)], column_sem)
    for h in range(2):
        value = from_column[h * NZL]
        for i in range(1, NZL):
            value += from_column[h * NZL + i]
        coeffs[core, here, h] = value

    for peer in across_peers + x_peers:
        send(coeffs.at[core, here], coeffs.at[core, here], plane_all_sem, peer, 2)
    send_snapshots(3)
    passed(coeffs.at[0, pl.ds(0, 15)], plane_all_sem)
    send(coeffs.at[core], coeffs.at[core], core_sem, other_core, 3)
    passed(coeffs.at[0], core_sem)

    rows = [
        coeffs[c_, y_ * NX + x_, h]
        for h in range(2) for x_ in range(NX) for y_ in range(NY) for c_ in range(NCORE)
    ]
    whole = jnp.concatenate(rows, axis=0)
    first = lax.broadcasted_iota(jnp.int32, whole.shape, 0) == 0
    energy_load.wait()
    scaled = jnp.where(first, 0.0, pltpu.roll(whole, 1, 0)) * energy_v[...]
    scaled_high, scaled_low = two_parts(scaled)
    weights[...] = (
        dot(vec_t[...], scaled_high, ALONG_LAST) + dot(vec_t[...], scaled_low, ALONG_LAST)
    ).astype(BF16)

    owner_zl = (z + 2) & 3
    side = ((z + 6 - owner_zl) & 7) >> 2
    owner_space = y * 8 + owner_zl * 2 + core

    def send_modes(c, offsets, group):
        start = pl.multiple_of((x * 2 + side) * piece + c * width, width)
        for d in offsets:
            to = tm ^ d
            send(
                rebuilt.at[c, pl.ds(pl.multiple_of(to * hours, hours), hours), :],
                modes.at[:, pl.ds(start, width)],
                modes_sem, (to, owner_space), group,
            )

    for c in range(CHUNKS):
        passed(gathered.at[c], snap_sem.at[c])
        rebuilt[c] = dot(weights[...], gathered[c]).astype(BF16)
        send_modes(c, CROSS_MODES, 4 + CHUNKS + c)

    whole_high, whole_low = two_parts(whole)
    operator[...] = (
        dot(whole_high, scaled_high, ALONG_FIRST)
        + dot(whole_high, scaled_low, ALONG_FIRST)
        + dot(whole_low, scaled_high, ALONG_FIRST)
    )

    for c in range(CHUNKS):
        passed(rebuilt.at[c, pl.ds(0, 6 * hours)], sent_sem.at[4 + CHUNKS + c])
        send_modes(c, SAME_MODES, 4 + 2 * CHUNKS)

    passed(parts.at[pl.ds(0, 7)], sent_sem.at[0])
    passed(from_column.at[pl.ds(0, 7)], sent_sem.at[1])
    passed(coeffs.at[0, pl.ds(0, 15)], sent_sem.at[2])
    passed(coeffs.at[0], sent_sem.at[3])
    for c in range(1, CHUNKS):
        passed(gathered.at[c], sent_sem.at[4 + c])
    passed(rebuilt.at[:, pl.ds(0, 2 * hours)], sent_sem.at[4 + 2 * CHUNKS])
    passed(modes, modes_sem)


def store_kernel(operator, modes, operator_out, modes_out, sems):
    step = modes.shape[1] // STORES
    copies = [
        pltpu.make_async_copy(modes.at[:, pl.ds(i * step, step)], modes_out.at[:, pl.ds(i * step, step)], sems.at[i])
        for i in range(STORES)
    ]
    copies.append(pltpu.make_async_copy(operator, operator_out, sems.at[STORES]))
    for copy in copies:
        copy.start()
    for copy in copies:
        copy.wait()


def per_device(eof_basis, snapshots, inverse_energy, eigen_vectors):
    cells, rank = eof_basis.shape
    hours = snapshots.shape[1]
    all_modes = eigen_vectors.shape[1]
    piece = cells // 8
    width = piece // CHUNKS
    anywhere = pl.BlockSpec(memory_space=pl.ANY)
    on_chip = pl.BlockSpec(memory_space=pltpu.VMEM)
    outputs = pl.pallas_call(
        kernel,
        out_shape=(pltpu.VMEM((rank, rank), F32), pltpu.VMEM((hours, cells), BF16)),
        in_specs=[anywhere] * 4,
        out_specs=(on_chip, on_chip),
        scratch_shapes=[
            pltpu.VMEM((cells, rank), BF16),
            pltpu.VMEM((hours, cells), BF16),
            pltpu.VMEM((rank, all_modes), BF16),
            pltpu.VMEM((all_modes, rank), BF16),
            pltpu.VMEM((8, 8, rank), F32),
            pltpu.VMEM((8, 8, rank), F32),
            pltpu.VMEM((NZ, 8, rank), F32),
            pltpu.VMEM((8, rank), F32),
            pltpu.VMEM((NCORE, NY * NX, 2, 8, rank), F32),
            pltpu.VMEM((CHUNKS, 8 * hours, width), BF16),
            pltpu.VMEM((all_modes, 8 * hours), BF16),
            pltpu.VMEM((CHUNKS, all_modes, width), BF16),
            pltpu.VMEM((1, rank), F32),
            pltpu.SemaphoreType.DMA((3 + K_CHUNKS,)),
            pltpu.SemaphoreType.DMA((5 + 2 * CHUNKS,)),
            pltpu.SemaphoreType.REGULAR((2,)),
            pltpu.SemaphoreType.DMA,
            pltpu.SemaphoreType.DMA,
            pltpu.SemaphoreType.DMA,
            pltpu.SemaphoreType.DMA,
            pltpu.SemaphoreType.DMA((CHUNKS,)),
            pltpu.SemaphoreType.DMA,
        ],
        compiler_params=pltpu.CompilerParams(
            collective_id=0, has_side_effects=True, vmem_limit_bytes=60 * 1024 * 1024
        ),
    )(eof_basis, snapshots.T, inverse_energy.reshape(1, rank), eigen_vectors)
    return pl.pallas_call(
        store_kernel,
        out_shape=(
            jax.ShapeDtypeStruct((rank, rank), F32),
            jax.ShapeDtypeStruct((hours, cells), BF16),
        ),
        in_specs=[on_chip, on_chip],
        out_specs=(anywhere, anywhere),
        scratch_shapes=[pltpu.SemaphoreType.DMA((STORES + 1,))],
    )(*[pltpu.with_memory_space_constraint(a, pltpu.VMEM) for a in outputs])


def solution(mesh):
    in_specs = (P("space", None), P("space", "tm"), P(), P())
    out_specs = (P(), P("tm", "space"))
    return jax.shard_map(
        per_device, mesh=mesh, in_specs=in_specs, out_specs=out_specs, check_vma=False
    )
```
